32 devices in a mesh: fsdp: 8 (over z, y), tp: 4 (over x, core).
Axes of the slice: x: 2, y: 2, z: 4, core: 2. Of those that a mesh axis runs over, the one named last changes fastest.
Arguments:
- block_input: bfloat16 [8, 1024, 768], P('fsdp', 'tp'), may hold values from -6 to 6
- out_grad: bfloat16 [8, 1024, 768], P('fsdp', 'tp'), may hold values from -6 to 6
- vectors: float32 [6, 768], replicated, may hold values from -1.5 to 1.7
- w_qkv: bfloat16 [3, 768, 768], P(None, 'fsdp', 'tp'), may hold values from -1.5 to 1.5
- query_value_bias: float32 [2, 768], P(None, 'tp'), may hold values from -3 to 3
- w_out: bfloat16 [768, 768], P('tp', 'fsdp'), may hold values from -0.875 to 0.875
- w_up: bfloat16 [768, 3072], P('fsdp', 'tp'), may hold values from -0.21875 to 0.21875
- up_bias: float32 [3072], P('tp'), may hold values from -3 to 3
- w_down: bfloat16 [3072, 768], P('tp', 'fsdp'), may hold values from -0.109375 to 0.109375
Outputs:
- block_output: bfloat16 [8, 1024, 768], P('fsdp', 'tp')
- input_grad: float32 [8, 1024, 768], P('fsdp', 'tp')
- vectors_grad: float32 [6, 768], P(None, ('fsdp', 'tp'))
- w_qkv_grad: float32 [3, 768, 768], P(None, 'fsdp', 'tp')
- bias_qv_grad: float32 [2, 768], P(None, ('tp', 'fsdp'))
- w_out_grad: float32 [768, 768], P('tp', 'fsdp')
- w_up_grad: float32 [768, 3072], P('fsdp', 'tp')
- b_up_grad: float32 [3072], P(('tp', 'fsdp'))
- w_down_grad: float32 [3072, 768], P('tp', 'fsdp')
The draws below stay inside these ranges and needn't reach their ends.
All inputs are finite; a program needn't handle non-finite values.
Results may differ from the reference program's by a relative error of at most 0.015.
Values may be sent and summed in bfloat16 or wider, within the bound.
No kernel may reach another device: no remote copies, remote signals or barrier semaphores. Data moves between devices by JAX's collectives and lax.ppermute only.
A program may use at most 128 MiB of HBM per device.

```python
import math
import jax
import jax.numpy as jnp
from jax import lax

D = 768
H = 12
HD = 64
FF = 3072
SEQ_LEN = 1024
SEQS = 8


def draw_vectors(key, part):
    key_gain, key_bias = jax.random.split(key)
    gains = jax.random.uniform(key_gain, (2, D), jnp.float32, 0.5, 1.5)
    shifts = 0.5 * jax.random.truncated_normal(key_bias, -3.0, 3.0, (4, D), jnp.float32)
    return jnp.stack([gains[0], shifts[0], shifts[1], gains[1], shifts[2], shifts[3]])


def draw_w_qkv(key, part):
    base = jax.random.truncated_normal(key, -4.0, 4.0, (3, D, D), jnp.float32) / math.sqrt(D)
    return base.astype(jnp.bfloat16)


def spiked(values, key, source, target, shards_of, factor):
    def block_of(axis_at):
        return (jnp.arange(values.shape[axis_at]) // (values.shape[axis_at] // shards_of)).reshape((-1,) + (1,) * (values.ndim - 1 - axis_at))

    one_side = jax.random.permutation(key, shards_of)[block_of(target)]
    far = (block_of(target) + shards_of // 2) % shards_of
    return jnp.where((block_of(source) == one_side) | (block_of(source) == far), factor * values, values)


def levels(own_key, dims, pieces, least, high):
    gain, own = 1.0, jax.random.fold_in(own_key, 6)
    for axis_at, blocks in pieces:
        steps = jnp.exp(jax.random.uniform(jax.random.fold_in(own, axis_at), (blocks,), jnp.float32, least / len(pieces), high / len(pieces)))
        gain = gain * jnp.repeat(steps, dims[axis_at] // blocks).reshape([-1 if axis == axis_at else 1 for axis in range(len(dims))])
    return gain


def noise(rng, extent, scale, most, shards=(), dtype=jnp.bfloat16):
    entries = scale * jax.random.normal(rng, extent, jnp.float32)
    if shards:
        entries = entries * levels(rng, extent, shards, -0.22, 0.18)
    return jnp.clip(entries, -most, most).astype(dtype)


def gaussian_with(rng, dims, scale, reach, shards, heavy, held_as=jnp.bfloat16):
    array = scale * jax.random.normal(rng, dims, jnp.float32)
    if shards:
        array = array * levels(rng, dims, shards, -0.22, 0.18)
    return jnp.clip(spiked(array, jax.random.fold_in(rng, 3), *heavy), -reach, reach).astype(held_as)


def setup_inputs(seed: int = 0) -> dict:
    arg_keys = jax.random.split(jax.random.key(seed), 10)
    block_input = noise(arg_keys[0], (SEQS, SEQ_LEN, D), 1.0, 6.0, ((0, 8), (1, 4)))
    out_grad = gaussian_with(arg_keys[1], (SEQS, SEQ_LEN, D), 1.0, 6.0, ((0, 8), (1, 4)), (0, 2, 8, 2.0))
    vectors = draw_vectors(jax.random.fold_in(arg_keys[9], 71), 0)
    w_qkv = draw_w_qkv(jax.random.fold_in(arg_keys[9], 71), 0)
    query_value_bias = noise(arg_keys[4], (2, D), 0.5, 3.0, ((1, 4),), jnp.float32)
    w_out = noise(arg_keys[5], (D, D), (D // 16) ** -0.5, 0.875, ((0, 4), (1, 8)))
    w_up = noise(arg_keys[6], (D, FF), D ** -0.5, 0.21875, ((0, 8), (1, 4)))
    up_bias = noise(arg_keys[7], (FF,), 0.5, 3.0, ((0, 4),), jnp.float32)
    w_down = noise(arg_keys[8], (FF, D), FF ** -0.5, 0.109375, ((0, 4), (1, 8)))
    return dict(block_input=block_input, out_grad=out_grad, vectors=vectors, w_qkv=w_qkv, query_value_bias=query_value_bias, w_out=w_out, w_up=w_up, up_bias=up_bias, w_down=w_down)


EPS = 1e-05
GELU_C = 0.7978845608028654
NEG_BIG = -1e+30

def rounded(arr):
    return lax.optimization_barrier(arr.astype(jnp.bfloat16))

def norm_fwd(rows_in, gain_row, bias_row):
    mean_row = lax.optimization_barrier(jnp.mean(rows_in, axis=-1, keepdims=True))
    centred = rows_in - mean_row
    inv_std = lax.rsqrt(lax.optimization_barrier(jnp.mean(centred * centred, axis=-1, keepdims=True)) + EPS)
    normed = centred * inv_std
    return (normed * gain_row + bias_row, normed, inv_std)

def norm_back(grad_out, normed, inv_std, gain_row):
    grad_hat = grad_out * gain_row
    grad_in = inv_std * (grad_hat - lax.optimization_barrier(jnp.mean(grad_hat, axis=-1, keepdims=True)) - normed * lax.optimization_barrier(jnp.mean(grad_hat * normed, axis=-1, keepdims=True)))
    width = grad_out.shape[-1]
    gain_grad = lax.optimization_barrier(jnp.sum((grad_out * normed).reshape(-1, width), axis=0))
    bias_grad = lax.optimization_barrier(jnp.sum(grad_out.reshape(-1, width), axis=0))
    return (grad_in, gain_grad, bias_grad)

def gelu_fwd(preactivation_values):
    inner_arg = GELU_C * (preactivation_values + 0.044715 * preactivation_values * preactivation_values * preactivation_values)
    return 0.5 * preactivation_values * (1.0 + jnp.tanh(inner_arg))

def gelu_slope(preactivation_values):
    inner_arg = GELU_C * (preactivation_values + 0.044715 * preactivation_values * preactivation_values * preactivation_values)
    tanh_val = jnp.tanh(inner_arg)
    return 0.5 * (1.0 + tanh_val) + 0.5 * preactivation_values * (1.0 - tanh_val * tanh_val) * GELU_C * (1.0 + 3.0 * 0.044715 * preactivation_values * preactivation_values)

def reference(block_input, out_grad, vectors, w_qkv, query_value_bias, w_out, w_up, up_bias, w_down):
    factor = 1.0 / math.sqrt(HD)
    causal = jnp.arange(SEQ_LEN)[:, None] >= jnp.arange(SEQ_LEN)[None, :]
    single_float = jnp.float32

    def one_seq(totals, seq_pair):
        seq_in, seq_grad = seq_pair
        in_f = seq_in.astype(single_float)
        attn_f, normed_a, inv_a = norm_fwd(in_f, vectors[0], vectors[1])
        attention_input = rounded(attn_f)
        query = rounded(jnp.dot(attention_input, w_qkv[0], preferred_element_type=single_float) + query_value_bias[0])
        random_keys = rounded(jnp.dot(attention_input, w_qkv[1], preferred_element_type=single_float))
        vals = rounded(jnp.dot(attention_input, w_qkv[2], preferred_element_type=single_float) + query_value_bias[1])
        query_heads = query.reshape(SEQ_LEN, H, HD).astype(single_float)
        key_heads = random_keys.reshape(SEQ_LEN, H, HD).astype(single_float)
        value_heads = vals.reshape(SEQ_LEN, H, HD).astype(single_float)
        scores = jnp.einsum('qhd,khd->hqk', query_heads, key_heads) * factor
        scores = jnp.where(causal, scores, NEG_BIG)
        log_norm = jax.nn.logsumexp(scores, axis=-1)
        prob_f = jnp.exp(scores - log_norm[..., None])
        prob_b = rounded(prob_f).astype(single_float)
        attention_output = rounded(jnp.einsum('hqk,khd->qhd', prob_b, value_heads).reshape(SEQ_LEN, D))
        resid = in_f + jnp.dot(attention_output, w_out, preferred_element_type=single_float) + vectors[2]
        mlp_f, normed_m, inv_m = norm_fwd(resid, vectors[3], vectors[4])
        feedforward_input = rounded(mlp_f)
        preactivation_values = jnp.dot(feedforward_input, w_up, preferred_element_type=single_float) + up_bias
        hidden_units = rounded(gelu_fwd(preactivation_values))
        out_rows = (resid + jnp.dot(hidden_units, w_down, preferred_element_type=single_float) + vectors[5]).astype(jnp.bfloat16)
        grad_f = seq_grad.astype(single_float)
        down_weight_gradient = jnp.dot(hidden_units.T, seq_grad, preferred_element_type=single_float)
        grad_pre = jnp.dot(seq_grad, w_down.T, preferred_element_type=single_float) * gelu_slope(preactivation_values)
        g_bup = lax.optimization_barrier(jnp.sum(grad_pre, axis=0))
        preactivation_gradient_local = rounded(grad_pre)
        up_weight_gradient = jnp.dot(feedforward_input.T, preactivation_gradient_local, preferred_element_type=single_float)
        grad_mlp = jnp.dot(preactivation_gradient_local, w_up.T, preferred_element_type=single_float)
        back_m, g_gain_two, g_bias_two = norm_back(grad_mlp, normed_m, inv_m, vectors[3])
        grad_resid = grad_f + back_m
        grad_resid_b = rounded(grad_resid)
        out_weight_gradient = jnp.dot(attention_output.T, grad_resid_b, preferred_element_type=single_float)
        attention_gradient = rounded(jnp.dot(grad_resid_b, w_out.T, preferred_element_type=single_float))
        grad_heads = attention_gradient.reshape(SEQ_LEN, H, HD).astype(single_float)
        out_heads = attention_output.reshape(SEQ_LEN, H, HD).astype(single_float)
        grad_delta = lax.optimization_barrier(jnp.sum(grad_heads * out_heads, axis=-1)).T
        grad_prob = jnp.einsum('qhd,khd->hqk', grad_heads, value_heads)
        grad_score = rounded(prob_f * (grad_prob - grad_delta[..., None]) * factor).astype(single_float)
        grad_query = jnp.einsum('hqk,khd->qhd', grad_score, key_heads).reshape(SEQ_LEN, D)
        grad_keys = jnp.einsum('hqk,qhd->khd', grad_score, query_heads).reshape(SEQ_LEN, D)
        grad_vals = jnp.einsum('hqk,qhd->khd', prob_b, grad_heads).reshape(SEQ_LEN, D)
        g_bqv = jnp.stack([lax.optimization_barrier(jnp.sum(grad_query, axis=0)), lax.optimization_barrier(jnp.sum(grad_vals, axis=0))])
        grad_parts = [rounded(grad_query), rounded(grad_keys), rounded(grad_vals)]
        query_key_value_gradient = jnp.stack([jnp.dot(attention_input.T, part_b, preferred_element_type=single_float) for part_b in grad_parts])
        grad_norm = jnp.dot(grad_parts[0], w_qkv[0].T, preferred_element_type=single_float)
        grad_norm = grad_norm + jnp.dot(grad_parts[1], w_qkv[1].T, preferred_element_type=single_float)
        grad_norm = grad_norm + jnp.dot(grad_parts[2], w_qkv[2].T, preferred_element_type=single_float)
        back_a, g_gain_one, g_bias_one = norm_back(grad_norm, normed_a, inv_a, vectors[0])
        grad_in = grad_resid + back_a
        g_vec = jnp.stack([g_gain_one, g_bias_one, lax.optimization_barrier(jnp.sum(grad_resid, axis=0)), g_gain_two, g_bias_two, lax.optimization_barrier(jnp.sum(grad_f, axis=0))])
        new_totals = (totals[0] + g_vec, totals[1] + query_key_value_gradient, totals[2] + g_bqv, totals[3] + out_weight_gradient, totals[4] + up_weight_gradient, totals[5] + g_bup, totals[6] + down_weight_gradient)
        return (new_totals, (out_rows, grad_in))
    init_totals = (jnp.zeros((6, D), single_float), jnp.zeros((3, D, D), single_float), jnp.zeros((2, D), single_float), jnp.zeros((D, D), single_float), jnp.zeros((D, FF), single_float), jnp.zeros((FF,), single_float), jnp.zeros((FF, D), single_float))
    totals, (out_all, grad_all) = lax.scan(one_seq, init_totals, (block_input, out_grad))
    return (out_all, grad_all, totals[0], totals[1], totals[2], totals[3], totals[4], totals[5], totals[6])
```

```python
import math

import jax
import jax.numpy as jnp
from jax import lax
from jax.sharding import PartitionSpec as P

HD = 64
EPS = 1e-05
GELU_C = 0.7978845608028654
NEG_BIG = -1e30
F32 = jnp.float32
BF16 = jnp.bfloat16


def norm_fwd(rows_in, gain_row, bias_row):
    mean_row = jnp.mean(rows_in, axis=-1, keepdims=True)
    centred = rows_in - mean_row
    inv_std = lax.rsqrt(jnp.mean(centred * centred, axis=-1, keepdims=True) + EPS)
    normed = centred * inv_std
    return (normed * gain_row + bias_row, normed, inv_std)


def norm_back(grad_out, normed, inv_std, gain_row):
    grad_hat = grad_out * gain_row
    return inv_std * (
        grad_hat
        - jnp.mean(grad_hat, axis=-1, keepdims=True)
        - normed * jnp.mean(grad_hat * normed, axis=-1, keepdims=True)
    )


def gelu_both(u):
    inner_arg = GELU_C * (u + 0.044715 * u * u * u)
    th = jnp.tanh(inner_arg)
    value = 0.5 * u * (1.0 + th)
    slope = 0.5 * (1.0 + th) + 0.5 * u * (1.0 - th * th) * GELU_C * (1.0 + 3.0 * 0.044715 * u * u)
    return value, slope


def dot(a, b, ca, cb):
    return lax.dot_general(a, b, (((ca,), (cb,)), ((), ())), preferred_element_type=F32)


def make_per_device(mesh):
    n_f = mesh.shape["fsdp"]
    n_t = mesh.shape["tp"]
    sizes = {"fsdp": n_f, "tp": n_t}

    def flip(v, axis, bit):
        return lax.ppermute(v, axis, [(i, i ^ bit) for i in range(sizes[axis])])

    def bits_down(n):
        out = []
        bit = n // 2
        while bit:
            out.append(bit)
            bit //= 2
        return out

    def gather_rows(v, axis):
        for bit in bits_down(sizes[axis]):
            v = jnp.concatenate([v, flip(v, axis, bit)], axis=0)
        return v

    def slot_ids(n):
        ids = [0]
        for bit in bits_down(n):
            ids = ids + [i ^ bit for i in ids]
        return ids

    def scatter_tp(v):
        for bit in reversed(bits_down(n_t)):
            half = v.shape[0] // 2
            got = flip(v[half:].astype(BF16), "tp", bit)
            v = v[:half] + got.astype(F32)
        return v

    def to_true(buf, own, n):
        ids = slot_ids(n)
        place = {s: k for k, s in enumerate(ids)}
        table = jnp.array([place[s] for s in range(n)], jnp.int32)
        return jnp.concatenate(
            [lax.dynamic_index_in_dim(buf, table[own ^ p], 0, keepdims=False) for p in range(n)], axis=0
        )

    def scatter_fsdp(v, own, wire):
        low = 1
        n = n_f
        while n > 1:
            bit = (own // low) % 2
            v = v.reshape((n // 2, 2) + v.shape[1:])
            keep = lax.dynamic_index_in_dim(v, bit, 1, keepdims=False)
            send = lax.dynamic_index_in_dim(v, 1 - bit, 1, keepdims=False).astype(wire)
            v = keep.astype(F32) + flip(send, "fsdp", low).astype(F32)
            if n > 2:
                v = v.astype(wire)
            n //= 2
            low *= 2
        return v[0]

    def per_device(block_input, out_grad, vectors, w_qkv, query_value_bias, w_out, w_up, up_bias, w_down):
        factor = 1.0 / math.sqrt(HD)
        width = block_input.shape[-1]
        x = block_input.reshape(-1, width)
        og = out_grad.reshape(-1, width)
        rows = x.shape[0]
        t = lax.axis_index("tp")
        f = lax.axis_index("fsdp")
        hcols = w_qkv.shape[2]
        heads = hcols // HD
        fcols = w_up.shape[1]
        drows = w_qkv.shape[1]

        pack_a = jnp.concatenate([w_qkv[0], w_qkv[1], w_qkv[2], w_out.T], axis=1)
        pack_b = jnp.concatenate([w_up, w_down.T], axis=1)

        xs = gather_rows(x, "tp")
        full_a = to_true(gather_rows(pack_a, "fsdp").reshape(n_f, drows, -1), f, n_f)
        full_b = to_true(gather_rows(pack_b, "fsdp").reshape(n_f, drows, -1), f, n_f)
        ogs = gather_rows(og, "tp")
        wqkv_full = full_a[:, : 3 * hcols]
        wout_t = full_a[:, 3 * hcols :]
        wup_full = full_b[:, :fcols]
        wdown_t = full_b[:, fcols:]

        slot_of = jnp.array(slot_ids(n_t), jnp.int32)
        pos = ((slot_of ^ t)[:, None] * rows + jnp.arange(rows)[None, :]).reshape(-1)
        causal = pos[:, None] >= pos[None, :]

        xf = xs.astype(F32)
        attn_f, normed_a, inv_a = norm_fwd(xf, vectors[0], vectors[1])
        attn_in = attn_f.astype(BF16)
        zeros = jnp.zeros((hcols,), F32)
        bias_all = jnp.concatenate([query_value_bias[0], zeros, query_value_bias[1]])
        qkv = (dot(attn_in, wqkv_full, 1, 0) + bias_all).astype(BF16)

        def head(a, k):
            return a[:, k * HD : (k + 1) * HD]

        outs = []
        saved = []
        for h in range(heads):
            q = head(qkv, h)
            k = head(qkv, heads + h)
            v = head(qkv, 2 * heads + h)
            s = jnp.where(causal, dot(q, k, 1, 1) * factor, NEG_BIG)
            top = jnp.max(s, axis=-1, keepdims=True)
            log_norm = top + jnp.log(jnp.sum(jnp.exp(s - top), axis=-1, keepdims=True))
            prob_b = jnp.exp(s - log_norm).astype(BF16)
            o = dot(prob_b, v, 1, 0).astype(BF16)
            outs.append(o)
            saved.append((q, k, v, log_norm, o))
        attn_out = jnp.concatenate(outs, axis=1)
        attn_proj = scatter_tp(dot(attn_out, wout_t, 1, 1))
        resid = x.astype(F32) + attn_proj + vectors[2]
        mlp_f, normed_m, inv_m = norm_fwd(resid, vectors[3], vectors[4])
        mlp_in = gather_rows(mlp_f.astype(BF16), "tp")
        pre_act = dot(mlp_in, wup_full, 1, 0) + up_bias
        value, slope = gelu_both(pre_act)
        hidden = value.astype(BF16)
        grad_pre = dot(ogs, wdown_t, 1, 0) * slope
        g_bup = jnp.sum(grad_pre, axis=0)
        grad_pre_b = grad_pre.astype(BF16)
        grad_mlp = scatter_tp(dot(grad_pre_b, wup_full, 1, 1))
        back_m = norm_back(grad_mlp, normed_m, inv_m, vectors[3])
        ogf = og.astype(F32)
        grad_resid = ogf + back_m
        gr = gather_rows(grad_resid.astype(BF16), "tp")

        mlp_proj = scatter_tp(dot(hidden, wdown_t, 1, 1))
        block_output = (resid + mlp_proj + vectors[5]).astype(BF16)
        g_down = dot(ogs, hidden, 0, 0).astype(BF16)
        g_up = dot(mlp_in, grad_pre_b, 0, 0).astype(BF16)
        up_grad = scatter_fsdp(g_up.reshape(n_f, drows, -1), f, BF16)
        down_grad = scatter_fsdp(g_down.reshape(n_f, drows, -1), f, BF16)

        g_out = dot(gr, attn_out, 0, 0).astype(BF16)
        grad_attn = dot(gr, wout_t, 1, 0).astype(BF16)
        dq, dk, dv = [], [], []
        for h in range(heads):
            q, k, v, log_norm, o = saved[h]
            g = head(grad_attn, h)
            delta = jnp.sum(g.astype(F32) * o.astype(F32), axis=-1, keepdims=True)
            s = jnp.where(causal, dot(q, k, 1, 1) * factor, NEG_BIG)
            prob_f = jnp.exp(s - log_norm)
            dv.append(dot(prob_f.astype(BF16), g, 0, 0))
            gs = (prob_f * (dot(g, v, 1, 1) - delta) * factor).astype(BF16)
            dq.append(dot(gs, k, 1, 0))
            dk.append(dot(gs, q, 0, 0))
        pile = jnp.concatenate(dq + dk + dv, axis=1)
        sums = jnp.sum(pile, axis=0)
        g_bqv = jnp.stack([sums[:hcols], sums[2 * hcols :]])
        pile_b = pile.astype(BF16)
        g_qkv = dot(attn_in, pile_b, 0, 0).astype(BF16)
        grad_norm_part = dot(pile_b, wqkv_full, 1, 1)
        g_gain_one = jnp.sum(grad_norm_part * normed_a, axis=0)
        g_bias_one = jnp.sum(grad_norm_part, axis=0)
        ga = jnp.concatenate([g_qkv, g_out], axis=1)
        a_grad = scatter_fsdp(ga.reshape(n_f, drows, -1), f, BF16)
        grad_norm = scatter_tp(grad_norm_part)
        back_a = norm_back(grad_norm, normed_a[:rows], inv_a[:rows], vectors[0])
        input_grad = grad_resid + back_a

        g_vec = jnp.stack(
            [
                g_gain_one,
                g_bias_one,
                jnp.sum(grad_resid, axis=0),
                jnp.sum(grad_mlp * normed_m, axis=0),
                jnp.sum(grad_mlp, axis=0),
                jnp.sum(ogf, axis=0),
            ]
        )
        small = jnp.concatenate(
            [
                jnp.transpose(g_vec.reshape(6, n_f, -1), (1, 0, 2)).reshape(n_f, -1),
                jnp.transpose(g_bqv.reshape(2, n_f, -1), (1, 0, 2)).reshape(n_f, -1),
                g_bup.reshape(n_f, -1),
            ],
            axis=1,
        )
        small = scatter_fsdp(small, f, F32)
        nv = 6 * drows
        nb = 2 * hcols // n_f
        bqv_grad = small[nv : nv + nb].reshape(2, -1)
        bup_grad = small[nv + nb :]
        vec = jnp.transpose(small[:nv].reshape(6, n_t, -1), (1, 0, 2))
        low = n_t // 2
        while low:
            bit = (t // low) % 2
            vec = vec.reshape((2, -1) + vec.shape[1:])
            keep = lax.dynamic_index_in_dim(vec, bit, 0, keepdims=False)
            send = lax.dynamic_index_in_dim(vec, 1 - bit, 0, keepdims=False)
            vec = keep + flip(send, "tp", low)
            low //= 2
        vectors_grad = vec[0]

        qkv_grad = jnp.stack([a_grad[:, k * hcols : (k + 1) * hcols] for k in range(3)])
        out_w_grad = a_grad[:, 3 * hcols :].T
        return (
            block_output.reshape(block_input.shape),
            input_grad.reshape(block_input.shape),
            vectors_grad,
            qkv_grad,
            bqv_grad,
            out_w_grad,
            up_grad,
            bup_grad,
            down_grad.T,
        )

    return per_device


def solution(mesh):
    placed = (
        P("fsdp", "tp", None),
        P("fsdp", "tp", None),
        P(),
        P(None, "fsdp", "tp"),
        P(None, "tp"),
        P("tp", "fsdp"),
        P("fsdp", "tp"),
        P("tp"),
        P("tp", "fsdp"),
    )
    return jax.shard_map(
        make_per_device(mesh),
        mesh=mesh,
        in_specs=placed,
        out_specs=(
            P("fsdp", "tp", None),
            P("fsdp", "tp", None),
            P(None, ("fsdp", "tp")),
            P(None, "fsdp", "tp"),
            P(None, ("tp", "fsdp")),
            P("tp", "fsdp"),
            P("fsdp", "tp"),
            P(("tp", "fsdp")),
            P("tp", "fsdp"),
        ),
        check_vma=False,
    )
```
